32 devices in a mesh: pairs: 8 (over y, x, core), blk: 4 (over z).
Axes of the slice: x: 2, y: 2, z: 4, core: 2. Of those that a mesh axis runs over, the one named last changes fastest.
Arguments:
- amplitudes: bfloat16 [128, 512, 512], P('pairs'), may hold values from -6 to 6
- chol_vectors: bfloat16 [4, 512, 512], P('blk'), may hold values from -0.25 to 0.25
- fock_vv: bfloat16 [512, 512], replicated, may hold values from -0.25 to 0.25
- occ_energy: float32 [128], replicated, may hold values from -2 to -0.5
- vir_energy: float32 [512], replicated, may hold values from 0.5 to 3
- pair_orbs: int32 [128, 2], P('pairs'), may hold values from 0 to 127, as said below
- live_count: int32 [8], P('pairs'), may hold values from 0 to 16, as said below
Outputs:
- update: bfloat16 [128, 512, 512], P('pairs', 'blk')
The draws below stay inside these ranges and needn't reach their ends.
Inputs may be any that keep to these rules, and one draw needn't show every extreme that they name: Owners p and q whose indices differ only in the highest bit of the owner index hold live_count[p] + live_count[q] = 16; some owner holds 16 live slots and its partner none. `pair_orbs`: each slot's orbitals satisfy i <= j.
All inputs are finite; a program needn't handle non-finite values.
Results may differ from the reference program's by a relative error of at most 0.0048.
Values may be sent and summed in bfloat16 or wider, within the bound.
A program may use at most 128 MiB of HBM per device.

```python
import jax
import jax.numpy as jnp
from jax import lax

V = 512
NO = 128
PAIRS_DEV = 8
CAP = 16
OWNERS = 8
SLOTS = 128
NCHOL = 4


def draw_live_count(key, part):
    half_owners = OWNERS // 2
    key_spread = jax.random.fold_in(key, 11)
    key_sign = jax.random.fold_in(key, 12)
    key_full = jax.random.fold_in(key, 13)
    spread = jax.random.randint(key_spread, (half_owners,), 0, PAIRS_DEV + 1)
    sign_draw = jax.random.randint(key_sign, (half_owners,), 0, 2) * 2 - 1
    full_owner = jax.random.randint(key_full, (), 0, half_owners)
    spread = jnp.where(jnp.arange(half_owners) == full_owner, PAIRS_DEV, spread)
    low_half = PAIRS_DEV + sign_draw * spread
    return jnp.concatenate([low_half, 2 * PAIRS_DEV - low_half]).astype(jnp.int32)


def draw_pair_orbs(key, part):
    key_first = jax.random.fold_in(key, 21)
    key_second = jax.random.fold_in(key, 22)
    first_orb = jax.random.randint(key_first, (SLOTS,), 0, NO)
    second_orb = jax.random.randint(key_second, (SLOTS,), first_orb, NO)
    return jnp.stack([first_orb, second_orb], axis=1).astype(jnp.int32)


def block_levels(key, extent, cuts, low, high):
    level = 1.0
    for position, shards_of in cuts:
        draws = jax.random.uniform(jax.random.fold_in(jax.random.fold_in(key, 6), position), (shards_of,), jnp.float32, low / len(cuts), high / len(cuts))
        level = level * jnp.repeat(jnp.exp(draws), extent[position] // shards_of).reshape((-1,) + (1,) * (len(extent) - 1 - position))
    return level


def bell_draw(key, shape, deviation, reach, pieces=(), kind=jnp.bfloat16):
    drawn = deviation * jax.random.normal(key, shape, jnp.float32)
    if pieces:
        drawn = drawn * block_levels(key, shape, pieces, -0.22, 0.18)
    return jnp.clip(drawn, -reach, reach).astype(kind)


def setup_inputs(seed: int = 0) -> dict:
    key_of = jax.random.split(jax.random.key(seed), 8)
    amplitudes = bell_draw(key_of[0], (SLOTS, V, V), 1.0, 6.0, ((0, 8),))
    chol_vectors = bell_draw(key_of[1], (NCHOL, V, V), V ** -0.5, 0.25, ((0, 4),))
    fock_vv = bell_draw(key_of[2], (V, V), V ** -0.5, 0.25)
    occ_energy = jnp.clip(jax.random.uniform(key_of[3], (NO,), jnp.float32, -2.0, -0.5), -2.0, -0.5)
    vir_energy = jnp.clip(jax.random.uniform(key_of[4], (V,), jnp.float32, 0.5, 3.0), 0.5, 3.0)
    pair_orbs = draw_pair_orbs(jax.random.fold_in(key_of[7], 71), 0)
    live_count = draw_live_count(jax.random.fold_in(key_of[7], 71), 0)
    return {"amplitudes": amplitudes, "chol_vectors": chol_vectors, "fock_vv": fock_vv, "occ_energy": occ_energy, "vir_energy": vir_energy, "pair_orbs": pair_orbs, "live_count": live_count}


def reference(amplitudes, chol_vectors, fock_vv, occ_energy, vir_energy, pair_orbs, live_count):
    amp_float = amplitudes.astype(jnp.float32)

    def add_vector(running, vector_bf):
        vector = vector_bf.astype(jnp.float32)
        partial_value = jnp.einsum("ac,scd->sad", vector, amp_float).astype(jnp.bfloat16)
        partial_value = lax.optimization_barrier(partial_value).astype(jnp.float32)
        return running + jnp.einsum("sad,bd->sab", partial_value, vector), None

    ladder, _ = lax.scan(add_vector, jnp.zeros(amp_float.shape, jnp.float32), chol_vectors)
    fock_float = fock_vv.astype(jnp.float32)
    residual = ladder + jnp.einsum("ac,scb->sab", fock_float, amp_float) + jnp.einsum("sac,bc->sab", amp_float, fock_float)
    occ_pair = occ_energy[pair_orbs]
    denominator = vir_energy[None, :, None] + vir_energy[None, None, :] - (occ_pair[:, 0] + occ_pair[:, 1])[:, None, None]
    slot_ids = jnp.arange(SLOTS, dtype=jnp.int32)
    owner_ids = slot_ids // CAP
    live_mask = (slot_ids % CAP) < live_count[owner_ids]
    return jnp.where(live_mask[:, None, None], residual / denominator, 0.0).astype(jnp.bfloat16)
```

```python
import functools

import jax
import jax.numpy as jnp
from jax import lax
from jax.experimental import pallas as pl
from jax.experimental.pallas import tpu as pltpu
from jax.sharding import PartitionSpec as P

NT = (((1,), (1,)), ((), ()))
Z_STEPS = (5, 10, 15)
P_STEP = 1


def flip(index, mask):
    out = index
    bit = 1
    while bit <= mask:
        if mask & bit:
            out = out + bit - 2 * bit * ((index // bit) % 2)
        bit *= 2
    return out


def kernel(
    owners, blocks, group,
    amp_hbm, chol_hbm, fock_hbm, occ_hbm, vir_hbm, orbs_hbm, live_hbm,
    out_ref,
    occ_ref, vir_ref, orbs_ref, live_ref,
    amp, vec, fcat, left, lhs, y_buf, acc, vcol,
    t_sem, in_sem, zs_sem, zr_sem, ps_sem, pr_sem, cs_sem, cr_sem,
):
    capacity, width, _ = amp_hbm.shape
    rows = width // blocks
    chips = owners // 2
    piece = width // owners
    n_groups = capacity // group
    own = lax.axis_index("pairs")
    blk = lax.axis_index("blk")
    chip = own // 2
    core = own % 2
    row0 = pl.multiple_of(blk * rows, rows)

    def at(pairs, block):
        return {"pairs": pairs, "blk": block}

    fock_copy = pltpu.make_async_copy(fock_hbm, fcat.at[:, pl.ds(0, width)], in_sem.at[0])
    own_copy = pltpu.make_async_copy(chol_hbm.at[0], fcat.at[:, pl.ds(width, width)], in_sem.at[1])

    def amp_copy(s):
        return pltpu.make_async_copy(amp_hbm.at[s], amp.at[s], t_sem.at[s])

    small_copies = [
        pltpu.make_async_copy(source, target, in_sem.at[2 + i])
        for i, (source, target) in enumerate(
            [(occ_hbm, occ_ref), (vir_hbm, vir_ref), (orbs_hbm, orbs_ref), (live_hbm, live_ref)])
    ]

    own_copy.start()
    fock_copy.start()
    for copy in small_copies:
        copy.start()
    for s in range(capacity):
        amp_copy(s).start()

    barrier = pltpu.get_barrier_semaphore()
    peers = [at(own, flip(blk, d)) for d in range(1, blocks)]
    peers += [at(flip(own, 2 * e), blk) for e in range(1, chips)]
    peers += [at(flip(own, 1), blk)]
    for peer in peers:
        pl.semaphore_signal(barrier, inc=1, device_id=peer, device_id_type=pl.DeviceIdType.MESH)
    pl.semaphore_wait(barrier, len(peers))

    def span(owner):
        return pl.ds(pl.multiple_of(owner * piece, piece), piece)

    def z_copy(d):
        return pltpu.make_async_remote_copy(
            src_ref=fcat.at[span(own), pl.ds(width, width)], dst_ref=vec.at[blk, span(own)],
            send_sem=zs_sem.at[d - 1], recv_sem=zr_sem.at[d - 1],
            device_id=at(own, flip(blk, d)), device_id_type=pl.DeviceIdType.MESH)

    def z_arrival(d):
        part = vec.at[flip(blk, d), span(own)]
        return pltpu.make_async_remote_copy(
            src_ref=part, dst_ref=part,
            send_sem=zs_sem.at[d - 1], recv_sem=zr_sem.at[d - 1],
            device_id=at(own, flip(blk, d)), device_id_type=pl.DeviceIdType.MESH)

    def p_copy(d, e, owner):
        part = vec.at[flip(blk, d), span(owner)]
        return pltpu.make_async_remote_copy(
            src_ref=part, dst_ref=part,
            send_sem=ps_sem.at[d - 1, e - 1], recv_sem=pr_sem.at[d - 1, e - 1],
            device_id=at(flip(own, 2 * e), blk), device_id_type=pl.DeviceIdType.MESH)

    def c_copy(d, e, owner):
        part = vec.at[flip(blk, d), span(owner)]
        return pltpu.make_async_remote_copy(
            src_ref=part, dst_ref=part,
            send_sem=cs_sem.at[d - 1, e], recv_sem=cr_sem.at[d - 1, e],
            device_id=at(flip(own, 1), blk), device_id_type=pl.DeviceIdType.MESH)

    def z_forward(d):
        z_arrival(d).wait_recv()
        for e in range(1, chips):
            p_copy(d, e, own).start()
        c_copy(d, 0, own).start()

    def p_forward(d):
        for e in range(1, chips):
            p_copy(d, e, flip(own, 2 * e)).wait_recv()
            c_copy(d, e, flip(own, 2 * e)).start()

    def c_arrival(d):
        for e in range(chips):
            c_copy(d, e, flip(flip(own, 1), 2 * e)).wait_recv()

    own_copy.wait()
    for d in range(1, blocks):
        z_copy(d).start()

    for copy in small_copies:
        copy.wait()

    row_ids = lax.broadcasted_iota(jnp.int32, (rows, width), 0) + row0
    col_ids = lax.broadcasted_iota(jnp.int32, (rows, width), 1)
    vcol[...] = jnp.sum(jnp.where(row_ids == col_ids, vir_ref[...], 0.0), axis=1, keepdims=True)

    fock_copy.wait()
    left[pl.ds(0, rows), :] = fcat[pl.ds(row0, rows), pl.ds(0, width)]
    left[pl.ds(rows, rows), :] = fcat[pl.ds(row0, rows), pl.ds(width, width)]

    hooks = {}

    def place(phase, step, action):
        hooks.setdefault(phase, {}).setdefault(step, []).append(action)

    z_steps = [min(capacity - 1, (capacity * k) // 16) for k in Z_STEPS]
    for d in range(1, blocks):
        if d <= len(z_steps):
            place(0, z_steps[d - 1], functools.partial(z_forward, d))
        else:
            place(d - 3, n_groups // 2, functools.partial(z_forward, d))
    place(0, capacity - 1, functools.partial(p_forward, 1))
    for d in range(2, blocks):
        place(d - 1, min(P_STEP, n_groups - 1), functools.partial(p_forward, d))

    def run_hooks(phase, step):
        for at_step, actions in hooks.get(phase, {}).items():
            @pl.when(step == at_step)
            def _(actions=actions):
                for action in actions:
                    action()

    def own_group(g, carry):
        for k in range(group):
            s = g * group + k
            pltpu.make_async_copy(amp_hbm.at[s], amp.at[s], t_sem.at[s]).wait()
            both = jnp.dot(left[...], amp[s], preferred_element_type=jnp.float32)
            acc[pl.ds(pl.multiple_of(s * rows, rows), rows), :] = both[:rows]
            lhs[pl.ds(k * rows, rows), pl.ds(width, width)] = both[rows:].astype(jnp.bfloat16)
            lhs[pl.ds(k * rows, rows), pl.ds(0, width)] = amp[s, pl.ds(row0, rows), :]
            run_hooks(0, s)
        here = pl.ds(pl.multiple_of(g * group * rows, group * rows), group * rows)
        acc[here, :] += lax.dot_general(lhs[...], fcat[...], NT, preferred_element_type=jnp.float32)
        return carry

    lax.fori_loop(0, n_groups, own_group, 0)

    for d in range(1, blocks):
        source = flip(blk, d)
        c_arrival(d)
        last = d == blocks - 1

        def vec_group(g, carry, d=d, source=source, last=last):
            for k in range(group):
                s = g * group + k
                y = jnp.dot(vec[source, pl.ds(row0, rows), :], amp[s], preferred_element_type=jnp.float32)
                y_buf[pl.ds(k * rows, rows), :] = y.astype(jnp.bfloat16)
            here = pl.ds(pl.multiple_of(g * group * rows, group * rows), group * rows)
            more = lax.dot_general(y_buf[...], vec[source], NT, preferred_element_type=jnp.float32)
            acc[here, :] += more
            if last:
                base = vcol[...] + vir_ref[...]
                for k in range(group):
                    s = g * group + k
                    occ = occ_ref[orbs_ref[0, s]] + occ_ref[orbs_ref[1, s]]
                    value = acc[pl.ds(pl.multiple_of(s * rows, rows), rows), :] / (base - occ)
                    live = jnp.full((rows, width), s, jnp.int32) < live_ref[0]
                    out_ref[s] = jnp.where(live, value, 0.0).astype(out_ref.dtype)
            run_hooks(d, g)
            return carry

        lax.fori_loop(0, n_groups, vec_group, 0)

    for d in range(1, blocks):
        z_copy(d).wait_send()
        for e in range(1, chips):
            p_copy(d, e, own).wait_send()
        c_copy(d, 0, own).wait_send()
        for e in range(1, chips):
            c_copy(d, e, flip(own, 2 * e)).wait_send()


def solution(mesh):
    owners = mesh.shape["pairs"]
    blocks = mesh.shape["blk"]

    def body(amplitudes, chol_vectors, fock_vv, occ_energy, vir_energy, pair_orbs, live_count):
        capacity, width, _ = amplitudes.shape
        rows = width // blocks
        chips = owners // 2
        group = min(4, capacity)
        dma = pltpu.SemaphoreType.DMA
        bf16, f32 = jnp.bfloat16, jnp.float32
        hbm = pl.BlockSpec(memory_space=pltpu.HBM)
        vmem = pl.BlockSpec(memory_space=pltpu.VMEM)
        return pl.pallas_call(
            functools.partial(kernel, owners, blocks, group),
            out_shape=pltpu.VMEM((capacity, rows, width), bf16),
            in_specs=[hbm] * 7,
            out_specs=vmem,
            scratch_shapes=[
                pltpu.SMEM(occ_energy.shape, f32),
                pltpu.VMEM((1, width), f32),
                pltpu.SMEM((2, capacity), jnp.int32),
                pltpu.SMEM(live_count.shape, jnp.int32),
                pltpu.VMEM((capacity, width, width), bf16),
                pltpu.VMEM((blocks, width, width), bf16),
                pltpu.VMEM((width, 2 * width), bf16),
                pltpu.VMEM((2 * rows, width), bf16),
                pltpu.VMEM((group * rows, 2 * width), bf16),
                pltpu.VMEM((group * rows, width), bf16),
                pltpu.VMEM((capacity * rows, width), f32),
                pltpu.VMEM((rows, 1), f32),
                dma((capacity,)), dma((6,)),
                dma((blocks - 1,)), dma((blocks - 1,)),
                dma((blocks - 1, chips)), dma((blocks - 1, chips)),
                dma((blocks - 1, chips)), dma((blocks - 1, chips)),
            ],
            compiler_params=pltpu.CompilerParams(
                collective_id=0, has_side_effects=True, vmem_limit_bytes=60 * 1024 * 1024),
        )(amplitudes, chol_vectors, fock_vv, occ_energy, vir_energy.reshape(1, width), pair_orbs.T, live_count)

    return jax.shard_map(
        body,
        mesh=mesh,
        in_specs=(
            P("pairs", None, None),
            P("blk", None, None),
            P(),
            P(),
            P(),
            P("pairs", None),
            P("pairs"),
        ),
        out_specs=P("pairs", "blk", None),
        check_vma=False,
    )
```

```python
import functools

import jax
import jax.numpy as jnp
from jax import lax
from jax.experimental import pallas as pl
from jax.experimental.pallas import tpu as pltpu
from jax.sharding import PartitionSpec as P

NT = (((1,), (1,)), ((), ()))
LINE_FAR = (1,)
BF16, F32 = jnp.bfloat16, jnp.float32
MESH = pl.DeviceIdType.MESH

def flip(index, mask):
    out = index
    bit = 1
    while bit <= mask:
        if mask & bit:
            out = out + bit - 2 * bit * ((index // bit) % 2)
        bit *= 2
    return out


def kernel(
    owners, blocks, shared,
    amp_hbm, chol_hbm, fock_hbm, occ_hbm, vir_hbm, orbs_hbm, live_hbm,
    out_ref,
    occ_ref, vir_ref, orbs_ref, live_ref,
    amp, vec, fock, left, y_buf, acc, inv, base,
    t_sem, in_sem, zs_sem, zr_sem, ps_sem, pr_sem, cs_sem, cr_sem,
):
    capacity, width, _ = amp_hbm.shape
    rows = width // blocks
    _, inner, chips, _, _, _ = vec.shape
    parts = inner.bit_length()
    own = lax.axis_index("pairs")
    blk = lax.axis_index("blk")
    chip, core = (own // 2, own % 2) if shared else (0, 0)
    row0 = pl.multiple_of(blk * rows, rows)
    def at(pairs, block):
        return {"pairs": pairs, "blk": block}

    barrier = pltpu.get_barrier_semaphore()
    peers = [at(own, flip(blk, d)) for d in range(1, blocks)]
    peers += [at(flip(own, 2 * e), blk) for e in range(1, chips)]
    peers += [at(flip(own, 1), blk)] * int(shared)
    for peer in peers:
        pl.semaphore_signal(barrier, inc=1, device_id=peer, device_id_type=MESH)

    own_copy = pltpu.make_async_copy(chol_hbm.at[0], vec.at[blk], in_sem.at[0])
    fock_copy = pltpu.make_async_copy(fock_hbm, fock, in_sem.at[1])
    small_copies = [
        pltpu.make_async_copy(source, target, in_sem.at[2 + i])
        for i, (source, target) in enumerate(
            [(occ_hbm, occ_ref), (vir_hbm, vir_ref), (orbs_hbm, orbs_ref), (live_hbm, live_ref)])
    ]

    def amp_copy(s):
        return pltpu.make_async_copy(amp_hbm.at[s], amp.at[s], t_sem.at[s])

    own_copy.start()
    fock_copy.start()
    for copy in small_copies:
        copy.start()
    for s in range(capacity):
        amp_copy(s).start()

    vector = [flip(blk, d) for d in range(blocks)]

    extents = [2 ** max(0, i - 1) for i in range(parts)]
    starts = [
        [flip(receiver // extent, min(1, i)) * extent if inner > 1 else 0 for i, extent in enumerate(extents)]
        for receiver in vector]
    chip_peers = [flip(chip, e) for e in range(chips)]
    own_peers = [flip(own, 2 * e) for e in range(chips)]
    twin, other = flip(own, 1), 1 - core

    def part(d, i):
        return pl.ds(starts[d][i], extents[i])

    def far(d):
        return [e for e in range(1, chips) if e & (e - 1)] if d in LINE_FAR else []

    def near(d):
        return [e for e in range(1, chips) if e not in far(d)]

    def line_copy(d, i, e=0):
        piece = vec.at[blk, part(d, i), chip_peers[e], core]
        return pltpu.make_async_remote_copy(
            src_ref=piece, dst_ref=piece, send_sem=zs_sem.at[d - 1, i, e], recv_sem=zr_sem.at[d - 1, i, e],
            device_id=at(own, vector[d]), device_id_type=MESH)

    def line_arrival(d, i, e=0):
        piece = vec.at[vector[d], part(0, i), chip_peers[e], core]
        return pltpu.make_async_remote_copy(
            src_ref=piece, dst_ref=piece, send_sem=zs_sem.at[d - 1, i, e], recv_sem=zr_sem.at[d - 1, i, e],
            device_id=at(own, vector[d]), device_id_type=MESH)

    def plane_copy(d, i, e, source):
        piece = vec.at[vector[d], part(0, i), source, core]
        return pltpu.make_async_remote_copy(
            src_ref=piece, dst_ref=piece, send_sem=ps_sem.at[d - 1, i, e - 1], recv_sem=pr_sem.at[d - 1, i, e - 1],
            device_id=at(own_peers[e], blk), device_id_type=MESH)

    def core_copy(d, i, side):
        piece = vec.at[vector[d], part(0, i), :, side]
        return pltpu.make_async_remote_copy(
            src_ref=piece, dst_ref=piece, send_sem=cs_sem.at[d - 1, i], recv_sem=cr_sem.at[d - 1, i],
            device_id=at(twin, blk), device_id_type=MESH)

    def open_line():
        pl.semaphore_wait(barrier, len(peers))
        for d in range(1, blocks):
            for e in [0] + far(d):
                line_copy(d, 0, e).start()
        for d in range(1, blocks):
            for i in range(1, parts):
                for e in [0] + far(d):
                    line_copy(d, i, e).start()

    def line_step(d, i):
        line_arrival(d, i).wait_recv()
        for e in near(d):
            plane_copy(d, i, e, chip).start()

    def plane_step(d, i):
        for e in far(d):
            line_arrival(d, i, e).wait_recv()
        for e in near(d):
            plane_copy(d, i, e, chip_peers[e]).wait_recv()
        core_copy(d, i, core).start()

    def core_step(d, i):
        core_copy(d, i, other).wait_recv()

    def rest(kind, d):
        return [(kind, d, i) for i in range(1, parts)]

    steps_left = [(line_step, d, 0) for d in range(1, blocks)] + rest(line_step, 1)
    for d in range(1, blocks):
        steps_left += [(plane_step, d, 0)] * int(shared) + rest(line_step, d + 1) * int(d + 1 < blocks)
        steps_left += [(core_step, d, 0)] * int(shared)
    for d in range(1, blocks):
        steps_left += rest(plane_step, d) + rest(core_step, d)

    def until(kind, d, i=0):
        i = min(i, parts - 1)
        if (kind, d, i) in steps_left:
            taken = steps_left.index((kind, d, i)) + 1
            for step, e, k in steps_left[:taken]:
                step(e, k)
            del steps_left[:taken]

    def phase(steps, body, hooks=()):
        def run(step, carry):
            body(step)
            for at_step, action in hooks:
                pl.when(step == min(at_step, steps - 1))(action)
            return carry

        lax.fori_loop(0, steps, run, 0)

    def span(step, size):
        return pl.ds(pl.multiple_of(step * size * rows, size * rows), size * rows)

    def whole(source):
        return vec[source].reshape(width, width)

    def rows_of(source):
        if shared:
            return vec[source, blk].reshape(rows, width)
        return vec[source, 0, 0, 0, pl.ds(row0, rows), :]

    for copy in small_copies:
        copy.wait()
    row_ids = lax.broadcasted_iota(jnp.int32, (rows, width), 0) + row0
    col_ids = lax.broadcasted_iota(jnp.int32, (rows, width), 1)
    vcol = jnp.sum(jnp.where(row_ids == col_ids, vir_ref[...], 0.0), axis=1, keepdims=True)
    base[...] = vcol + vir_ref[...]
    fock_copy.wait()
    left[pl.ds(0, rows), :] = fock[pl.ds(row0, rows), :]

    quad, octo, many = min(4, capacity), min(8, capacity), min(16, capacity)

    def own_left(step):
        for k in range(quad):
            amp_copy(step * quad + k).wait()
        for k in range(quad):
            s = step * quad + k
            both = jnp.dot(left[pl.ds(0, 2 * rows), :], amp[s], preferred_element_type=F32)
            here = pl.ds(pl.multiple_of(s * rows, rows), rows)
            acc[here, :] = both[:rows]
            y_buf[0, here, :] = both[rows:].astype(BF16)
            occ = occ_ref[orbs_ref[0, s]] + occ_ref[orbs_ref[1, s]]
            live = jnp.full((rows, width), s, jnp.int32) < live_ref[0]
            inv[here, :] = jnp.where(live, 1.0 / (base[...] - occ), 0.0)

    def own_right(step):
        here = span(step, octo)
        mine = amp[pl.ds(step * octo, octo), pl.ds(row0, rows), :].reshape(octo * rows, width)
        more = lax.dot_general(mine, fock[...], NT, preferred_element_type=F32)
        more += lax.dot_general(y_buf[0, here, :], whole(blk), NT, preferred_element_type=F32)
        acc[here, :] += more

    own_copy.wait()
    left[pl.ds(rows, rows), :] = rows_of(blk)
    open_line()
    phase(capacity // quad, own_left, [(3, functools.partial(until, line_step, 1, 0))])
    phase(capacity // octo, own_right, [(0, functools.partial(until, line_step, 2, 0)), (1, functools.partial(until, line_step, 3, 0))])

    for d in range(1, blocks):
        until(line_step, d)
        until(core_step, d)
        left[pl.ds(0, rows), :] = rows_of(vector[d])

        def lefts(step, d=d):
            for k in range(octo):
                s = step * octo + k
                y = jnp.dot(left[pl.ds(0, rows), :], amp[s], preferred_element_type=F32)
                y_buf[d - 1, pl.ds(pl.multiple_of(s * rows, rows), rows), :] = y.astype(BF16)

        if d < blocks - 1:
            hooks = [(plane_step, d + 1, 0), (core_step, d + 1, 0)]
        else:
            hooks = [(plane_step, 1, parts), (plane_step, 2, parts)]
        phase(capacity // octo, lefts, [(k, functools.partial(until, *hook)) for k, hook in enumerate(hooks)])

    for d in range(1, blocks):
        last = d == blocks - 1
        until(core_step, d, parts)

        def rights(step, d=d, last=last):
            here = span(step, many)
            more = lax.dot_general(y_buf[d - 1, here, :], whole(vector[d]), NT, preferred_element_type=F32)
            if last:
                value = ((acc[here, :] + more) * inv[here, :]).astype(BF16)
                out_ref[pl.ds(step * many, many)] = value.reshape(many, rows, width)
            else:
                acc[here, :] += more

        phase(capacity // many, rights)
        until(plane_step, d + 2, parts)

    for d in range(1, blocks):
        for i in range(parts):
            for e in [0] + far(d):
                line_copy(d, i, e).wait_send()
            for e in near(d):
                plane_copy(d, i, e, chip).wait_send()
            if shared:
                core_copy(d, i, core).wait_send()


def solution(mesh):
    owners = mesh.shape["pairs"]
    blocks = mesh.shape["blk"]

    def body(amplitudes, chol_vectors, fock_vv, occ_energy, vir_energy, pair_orbs, live_count):
        capacity, width, _ = amplitudes.shape
        rows = width // blocks
        shared = rows % (16 * owners) == 0
        view = (blocks, owners // 2, 2, rows // owners, width) if shared else (1, 1, 1, width, width)
        parts = view[0].bit_length()
        dma = pltpu.SemaphoreType.DMA
        hbm = pl.BlockSpec(memory_space=pltpu.HBM)
        vmem = pl.BlockSpec(memory_space=pltpu.VMEM)
        n_sends = max(1, view[1] - 1)
        return pl.pallas_call(
            functools.partial(kernel, owners, blocks, shared),
            out_shape=pltpu.VMEM((capacity, rows, width), BF16),
            in_specs=[hbm] * 7,
            out_specs=vmem,
            scratch_shapes=[
                pltpu.SMEM(occ_energy.shape, F32),
                pltpu.VMEM((1, width), F32),
                pltpu.SMEM((2, capacity), jnp.int32),
                pltpu.SMEM(live_count.shape, jnp.int32),
                pltpu.VMEM((capacity, width, width), BF16),
                pltpu.VMEM((blocks,) + view, BF16),
                pltpu.VMEM((width, width), BF16),
                pltpu.VMEM((2 * rows, width), BF16),
                pltpu.VMEM((blocks - 1, capacity * rows, width), BF16),
                pltpu.VMEM((capacity * rows, width), F32),
                pltpu.VMEM((capacity * rows, width), F32),
                pltpu.VMEM((rows, width), F32),
                dma((capacity,)), dma((6,)),
                dma((blocks - 1, parts, n_sends + 1)), dma((blocks - 1, parts, n_sends + 1)),
                dma((blocks - 1, parts, n_sends)), dma((blocks - 1, parts, n_sends)),
                dma((blocks - 1, parts)), dma((blocks - 1, parts)),
            ],
            compiler_params=pltpu.CompilerParams(
                collective_id=0, has_side_effects=True, vmem_limit_bytes=60000 * 1024),
        )(amplitudes, chol_vectors.reshape((1,) + view), fock_vv, occ_energy,
          vir_energy.reshape(1, width), pair_orbs.T, live_count)

    return jax.shard_map(
        body,
        mesh=mesh,
        in_specs=(
            P("pairs", None, None),
            P("blk", None, None),
            P(),
            P(),
            P(),
            P("pairs", None),
            P("pairs"),
        ),
        out_specs=P("pairs", "blk", None),
        check_vma=False,
    )
```

```python
import functools

import jax
import jax.numpy as jnp
from jax import lax
from jax.experimental import pallas as pl
from jax.experimental.pallas import tpu as pltpu
from jax.sharding import PartitionSpec as P

NT = (((1,), (1,)), ((), ()))
LINE_FAR = (1,)
BF16, F32 = jnp.bfloat16, jnp.float32
MESH = pl.DeviceIdType.MESH

def flip(index, mask):
    out = index
    bit = 1
    while bit <= mask:
        if mask & bit:
            out = out + bit - 2 * bit * ((index // bit) % 2)
        bit *= 2
    return out


def kernel(
    owners, blocks, shared,
    amp_hbm, chol_hbm, fock_hbm, occ_hbm, vir_hbm, orbs_hbm, live_hbm,
    out_ref,
    occ_ref, vir_ref, orbs_ref, live_ref,
    amp, vec, fock, left, y_buf, acc, inv, base,
    t_sem, in_sem, zs_sem, zr_sem, ps_sem, pr_sem, cs_sem, cr_sem,
):
    capacity, width, _ = amp_hbm.shape
    rows = width // blocks
    _, inner, chips, _, _, _ = vec.shape
    parts = inner.bit_length()
    own = lax.axis_index("pairs")
    blk = lax.axis_index("blk")
    chip, core = (own // 2, own % 2) if shared else (0, 0)
    row0 = pl.multiple_of(blk * rows, rows)
    def at(pairs, block):
        return {"pairs": pairs, "blk": block}

    barrier = pltpu.get_barrier_semaphore()
    peers = [at(own, flip(blk, d)) for d in range(1, blocks)]
    peers += [at(flip(own, 2 * e), blk) for e in range(1, chips)]
    peers += [at(flip(own, 1), blk)] * int(shared)
    for peer in peers:
        pl.semaphore_signal(barrier, inc=1, device_id=peer, device_id_type=MESH)

    own_copy = pltpu.make_async_copy(chol_hbm.at[0], vec.at[blk], in_sem.at[0])
    fock_copy = pltpu.make_async_copy(fock_hbm, fock, in_sem.at[1])
    small_copies = [
        pltpu.make_async_copy(source, target, in_sem.at[2 + i])
        for i, (source, target) in enumerate(
            [(occ_hbm, occ_ref), (vir_hbm, vir_ref), (orbs_hbm, orbs_ref), (live_hbm, live_ref)])
    ]

    def amp_copy(s):
        return pltpu.make_async_copy(amp_hbm.at[s], amp.at[s], t_sem.at[s])

    own_copy.start()
    fock_copy.start()
    for copy in small_copies:
        copy.start()
    for s in range(capacity):
        amp_copy(s).start()

    vector = [flip(blk, d) for d in range(blocks)]

    extents = [2 ** max(0, i - 1) for i in range(parts)]
    starts = [
        [flip(receiver // extent, min(1, i)) * extent if inner > 1 else 0 for i, extent in enumerate(extents)]
        for receiver in vector]
    chip_peers = [flip(chip, e) for e in range(chips)]
    own_peers = [flip(own, 2 * e) for e in range(chips)]
    twin, other = flip(own, 1), 1 - core

    def part(d, i):
        return pl.ds(starts[d][i], extents[i])

    def far(d):
        return [e for e in range(1, chips) if e & (e - 1)] if d in LINE_FAR else []

    def near(d):
        return [e for e in range(chips - 1, 0, -1) if e not in far(d)]

    def line_copy(d, i, e=0):
        piece = vec.at[blk, part(d, i), chip_peers[e], core]
        return pltpu.make_async_remote_copy(
            src_ref=piece, dst_ref=piece, send_sem=zs_sem.at[d - 1, i, e], recv_sem=zr_sem.at[d - 1, i, e],
            device_id=at(own, vector[d]), device_id_type=MESH)

    def line_arrival(d, i, e=0):
        piece = vec.at[vector[d], part(0, i), chip_peers[e], core]
        return pltpu.make_async_remote_copy(
            src_ref=piece, dst_ref=piece, send_sem=zs_sem.at[d - 1, i, e], recv_sem=zr_sem.at[d - 1, i, e],
            device_id=at(own, vector[d]), device_id_type=MESH)

    def plane_copy(d, i, e, source):
        piece = vec.at[vector[d], part(0, i), source, core]
        return pltpu.make_async_remote_copy(
            src_ref=piece, dst_ref=piece, send_sem=ps_sem.at[d - 1, i, e - 1], recv_sem=pr_sem.at[d - 1, i, e - 1],
            device_id=at(own_peers[e], blk), device_id_type=MESH)

    def core_copy(d, i, side):
        piece = vec.at[vector[d], part(0, i), :, side]
        return pltpu.make_async_remote_copy(
            src_ref=piece, dst_ref=piece, send_sem=cs_sem.at[d - 1, i], recv_sem=cr_sem.at[d - 1, i],
            device_id=at(twin, blk), device_id_type=MESH)

    def open_line():
        pl.semaphore_wait(barrier, len(peers))
        for d in range(1, blocks):
            for e in [0] + far(d):
                line_copy(d, 0, e).start()
        for d in range(1, blocks):
            for i in range(1, parts):
                for e in [0] + far(d):
                    line_copy(d, i, e).start()

    def line_step(d, i):
        line_arrival(d, i).wait_recv()
        for e in near(d):
            plane_copy(d, i, e, chip).start()

    def plane_step(d, i):
        for e in far(d):
            line_arrival(d, i, e).wait_recv()
        for e in near(d):
            plane_copy(d, i, e, chip_peers[e]).wait_recv()
        core_copy(d, i, core).start()

    def core_step(d, i):
        core_copy(d, i, other).wait_recv()

    def rest(kind, d):
        return [(kind, d, i) for i in range(1, parts)]

    steps_left = [(line_step, d, 0) for d in range(1, blocks)] + rest(line_step, 1)
    for d in range(1, blocks):
        steps_left += [(plane_step, d, 0)] * int(shared) + rest(line_step, d + 1) * int(d + 1 < blocks)
        steps_left += [(core_step, d, 0)] * int(shared)
    for d in range(1, blocks):
        steps_left += rest(plane_step, d) + rest(core_step, d)

    def until(kind, d, i=0):
        i = min(i, parts - 1)
        if (kind, d, i) in steps_left:
            taken = steps_left.index((kind, d, i)) + 1
            for step, e, k in steps_left[:taken]:
                step(e, k)
            del steps_left[:taken]

    def phase(steps, body, hooks=()):
        def run(step, carry):
            body(step)
            for at_step, action in hooks:
                pl.when(step == min(at_step, steps - 1))(action)
            return carry

        lax.fori_loop(0, steps, run, 0)

    def span(step, size):
        return pl.ds(pl.multiple_of(step * size * rows, size * rows), size * rows)

    def whole(source):
        return vec[source].reshape(width, width)

    def rows_of(source):
        if shared:
            return vec[source, blk].reshape(rows, width)
        return vec[source, 0, 0, 0, pl.ds(row0, rows), :]

    for copy in small_copies:
        copy.wait()
    row_ids = lax.broadcasted_iota(jnp.int32, (rows, width), 0) + row0
    col_ids = lax.broadcasted_iota(jnp.int32, (rows, width), 1)
    vcol = jnp.sum(jnp.where(row_ids == col_ids, vir_ref[...], 0.0), axis=1, keepdims=True)
    base[...] = vcol + vir_ref[...]
    fock_copy.wait()
    left[pl.ds(0, rows), :] = fock[pl.ds(row0, rows), :]

    quad, octo, many = min(4, capacity), min(8, capacity), min(16, capacity)

    def own_left(step):
        for k in range(quad):
            amp_copy(step * quad + k).wait()
        for k in range(quad):
            s = step * quad + k
            both = jnp.dot(left[pl.ds(0, 2 * rows), :], amp[s], preferred_element_type=F32)
            here = pl.ds(pl.multiple_of(s * rows, rows), rows)
            acc[here, :] = both[:rows]
            y_buf[0, here, :] = both[rows:].astype(BF16)
            occ = occ_ref[orbs_ref[0, s]] + occ_ref[orbs_ref[1, s]]
            live = jnp.full((rows, width), s, jnp.int32) < live_ref[0]
            inv[here, :] = jnp.where(live, 1.0 / (base[...] - occ), 0.0)

    def own_right(step):
        here = span(step, octo)
        mine = amp[pl.ds(step * octo, octo), pl.ds(row0, rows), :].reshape(octo * rows, width)
        more = lax.dot_general(mine, fock[...], NT, preferred_element_type=F32)
        more += lax.dot_general(y_buf[0, here, :], whole(blk), NT, preferred_element_type=F32)
        acc[here, :] += more

    own_copy.wait()
    left[pl.ds(rows, rows), :] = rows_of(blk)
    open_line()
    phase(capacity // quad, own_left, [(3, functools.partial(until, line_step, 1, 0))])
    phase(capacity // octo, own_right, [(0, functools.partial(until, line_step, 2, 0)), (1, functools.partial(until, line_step, 3, 0))])

    for d in range(1, blocks):
        until(line_step, d)
        until(core_step, d)
        left[pl.ds(0, rows), :] = rows_of(vector[d])

        def lefts(step, d=d):
            for k in range(octo):
                s = step * octo + k
                y = jnp.dot(left[pl.ds(0, rows), :], amp[s], preferred_element_type=F32)
                y_buf[d - 1, pl.ds(pl.multiple_of(s * rows, rows), rows), :] = y.astype(BF16)

        if d < blocks - 1:
            hooks = [(plane_step, d + 1, 0), (core_step, d + 1, 0)]
        else:
            hooks = [(plane_step, 1, parts), (plane_step, 2, parts)]
        phase(capacity // octo, lefts, [(k, functools.partial(until, *hook)) for k, hook in enumerate(hooks)])

    for d in range(1, blocks):
        last = d == blocks - 1
        until(core_step, d, parts)

        def rights(step, d=d, last=last):
            here = span(step, many)
            more = lax.dot_general(y_buf[d - 1, here, :], whole(vector[d]), NT, preferred_element_type=F32)
            if last:
                value = ((acc[here, :] + more) * inv[here, :]).astype(BF16)
                out_ref[pl.ds(step * many, many)] = value.reshape(many, rows, width)
            else:
                acc[here, :] += more

        phase(capacity // many, rights)
        until(plane_step, d + 2, parts)

    for d in range(1, blocks):
        for i in range(parts):
            for e in [0] + far(d):
                line_copy(d, i, e).wait_send()
            for e in near(d):
                plane_copy(d, i, e, chip).wait_send()
            if shared:
                core_copy(d, i, core).wait_send()


def solution(mesh):
    owners = mesh.shape["pairs"]
    blocks = mesh.shape["blk"]

    def body(amplitudes, chol_vectors, fock_vv, occ_energy, vir_energy, pair_orbs, live_count):
        capacity, width, _ = amplitudes.shape
        rows = width // blocks
        shared = rows % (16 * owners) == 0
        view = (blocks, owners // 2, 2, rows // owners, width) if shared else (1, 1, 1, width, width)
        parts = view[0].bit_length()
        dma = pltpu.SemaphoreType.DMA
        hbm = pl.BlockSpec(memory_space=pltpu.HBM)
        vmem = pl.BlockSpec(memory_space=pltpu.VMEM)
        n_sends = max(1, view[1] - 1)
        return pl.pallas_call(
            functools.partial(kernel, owners, blocks, shared),
            out_shape=pltpu.VMEM((capacity, rows, width), BF16),
            in_specs=[hbm] * 7,
            out_specs=vmem,
            scratch_shapes=[
                pltpu.SMEM(occ_energy.shape, F32),
                pltpu.VMEM((1, width), F32),
                pltpu.SMEM((2, capacity), jnp.int32),
                pltpu.SMEM(live_count.shape, jnp.int32),
                pltpu.VMEM((capacity, width, width), BF16),
                pltpu.VMEM((blocks,) + view, BF16),
                pltpu.VMEM((width, width), BF16),
                pltpu.VMEM((2 * rows, width), BF16),
                pltpu.VMEM((blocks - 1, capacity * rows, width), BF16),
                pltpu.VMEM((capacity * rows, width), F32),
                pltpu.VMEM((capacity * rows, width), F32),
                pltpu.VMEM((rows, width), F32),
                dma((capacity,)), dma((6,)),
                dma((blocks - 1, parts, n_sends + 1)), dma((blocks - 1, parts, n_sends + 1)),
                dma((blocks - 1, parts, n_sends)), dma((blocks - 1, parts, n_sends)),
                dma((blocks - 1, parts)), dma((blocks - 1, parts)),
            ],
            compiler_params=pltpu.CompilerParams(
                collective_id=0, has_side_effects=True, vmem_limit_bytes=60000 * 1024),
        )(amplitudes, chol_vectors.reshape((1,) + view), fock_vv, occ_energy,
          vir_energy.reshape(1, width), pair_orbs.T, live_count)

    return jax.shard_map(
        body,
        mesh=mesh,
        in_specs=(
            P("pairs", None, None),
            P("blk", None, None),
            P(),
            P(),
            P(),
            P("pairs", None),
            P("pairs"),
        ),
        out_specs=P("pairs", "blk", None),
        check_vma=False,
    )
```

```python
import functools

import jax
import jax.numpy as jnp
from jax import lax
from jax.experimental import pallas as pl
from jax.experimental.pallas import tpu as pltpu
from jax.sharding import PartitionSpec as P

NT = (((1,), (1,)), ((), ()))
LINE_FAR = (1,)
BF16, F32 = jnp.bfloat16, jnp.float32
MESH = pl.DeviceIdType.MESH

def flip(index, mask):
    out = index
    bit = 1
    while bit <= mask:
        if mask & bit:
            out = out + bit - 2 * bit * ((index // bit) % 2)
        bit *= 2
    return out


def kernel(
    owners, blocks, shared,
    amp_hbm, chol_hbm, fock_hbm, occ_hbm, vir_hbm, orbs_hbm, live_hbm,
    out_ref,
    occ_ref, vir_ref, orbs_ref, live_ref,
    amp, vec, fock, left, y_buf, acc, inv, base,
    t_sem, in_sem, zs_sem, zr_sem, ps_sem, pr_sem, cs_sem, cr_sem,
):
    capacity, width, _ = amp_hbm.shape
    rows = width // blocks
    _, inner, chips, _, _, _ = vec.shape
    parts = inner.bit_length()
    own = lax.axis_index("pairs")
    blk = lax.axis_index("blk")
    chip, core = (own // 2, own % 2) if shared else (0, 0)
    row0 = pl.multiple_of(blk * rows, rows)
    def at(pairs, block):
        return {"pairs": pairs, "blk": block}

    barrier = pltpu.get_barrier_semaphore()
    peers = [at(own, flip(blk, d)) for d in range(1, blocks)]
    peers += [at(flip(own, 2 * e), blk) for e in range(1, chips)]
    peers += [at(flip(own, 1), blk)] * int(shared)
    for peer in peers:
        pl.semaphore_signal(barrier, inc=1, device_id=peer, device_id_type=MESH)

    own_copy = pltpu.make_async_copy(chol_hbm.at[0], vec.at[blk], in_sem.at[0])
    fock_copy = pltpu.make_async_copy(fock_hbm, fock, in_sem.at[1])
    small_copies = [
        pltpu.make_async_copy(source, target, in_sem.at[2 + i])
        for i, (source, target) in enumerate(
            [(occ_hbm, occ_ref), (vir_hbm, vir_ref), (orbs_hbm, orbs_ref), (live_hbm, live_ref)])
    ]

    def amp_copy(s):
        return pltpu.make_async_copy(amp_hbm.at[s], amp.at[s], t_sem.at[s])

    own_copy.start()
    fock_copy.start()
    for copy in small_copies:
        copy.start()
    for s in range(capacity):
        amp_copy(s).start()

    vector = [flip(blk, d) for d in range(blocks)]

    extents = [2 ** max(0, i - 1) for i in range(parts)]
    starts = [
        [flip(receiver // extent, min(1, i)) * extent if inner > 1 else 0 for i, extent in enumerate(extents)]
        for receiver in vector]
    chip_peers = [flip(chip, e) for e in range(chips)]
    own_peers = [flip(own, 2 * e) for e in range(chips)]
    twin, other = flip(own, 1), 1 - core

    def part(d, i):
        return pl.ds(starts[d][i], extents[i])

    def far(d):
        return [e for e in range(1, chips) if e & (e - 1)] if d in LINE_FAR else []

    def near(d):
        return [e for e in range(chips - 1, 0, -1) if e not in far(d)]

    def line_copy(d, i, e=0):
        piece = vec.at[blk, part(d, i), chip_peers[e], core]
        return pltpu.make_async_remote_copy(
            src_ref=piece, dst_ref=piece, send_sem=zs_sem.at[d - 1, i, e], recv_sem=zr_sem.at[d - 1, i, e],
            device_id=at(own, vector[d]), device_id_type=MESH)

    def line_arrival(d, i, e=0):
        piece = vec.at[vector[d], part(0, i), chip_peers[e], core]
        return pltpu.make_async_remote_copy(
            src_ref=piece, dst_ref=piece, send_sem=zs_sem.at[d - 1, i, e], recv_sem=zr_sem.at[d - 1, i, e],
            device_id=at(own, vector[d]), device_id_type=MESH)

    def plane_copy(d, i, e, source):
        piece = vec.at[vector[d], part(0, i), source, core]
        return pltpu.make_async_remote_copy(
            src_ref=piece, dst_ref=piece, send_sem=ps_sem.at[d - 1, i, e - 1], recv_sem=pr_sem.at[d - 1, i, e - 1],
            device_id=at(own_peers[e], blk), device_id_type=MESH)

    def core_copy(d, i, side):
        piece = vec.at[vector[d], part(0, i), :, side]
        return pltpu.make_async_remote_copy(
            src_ref=piece, dst_ref=piece, send_sem=cs_sem.at[d - 1, i], recv_sem=cr_sem.at[d - 1, i],
            device_id=at(twin, blk), device_id_type=MESH)

    def open_line():
        pl.semaphore_wait(barrier, len(peers))
        for d in range(1, blocks):
            for e in [0] + far(d):
                line_copy(d, 0, e).start()
        for d in range(1, blocks):
            for i in range(1, parts):
                for e in [0] + far(d):
                    line_copy(d, i, e).start()

    def line_step(d, i):
        line_arrival(d, i).wait_recv()
        for e in near(d):
            plane_copy(d, i, e, chip).start()

    def plane_step(d, i):
        for e in far(d):
            line_arrival(d, i, e).wait_recv()
        for e in near(d):
            plane_copy(d, i, e, chip_peers[e]).wait_recv()
        core_copy(d, i, core).start()

    def core_step(d, i):
        core_copy(d, i, other).wait_recv()

    def rest(kind, d):
        return [(kind, d, i) for i in range(1, parts)]

    steps_left = [(line_step, d, 0) for d in range(1, blocks)] + rest(line_step, 1)
    for d in range(1, blocks):
        steps_left += [(plane_step, d, 0)] * int(shared) + rest(line_step, d + 1) * int(d + 1 < blocks)
        steps_left += [(core_step, d, 0)] * int(shared)
    for d in range(1, blocks):
        steps_left += rest(plane_step, d) + rest(core_step, d)

    def until(kind, d, i=0):
        i = min(i, parts - 1)
        if (kind, d, i) in steps_left:
            taken = steps_left.index((kind, d, i)) + 1
            for step, e, k in steps_left[:taken]:
                step(e, k)
            del steps_left[:taken]

    def phase(steps, body, hooks=()):
        def run(step, carry):
            body(step)
            for at_step, action in hooks:
                pl.when(step == min(at_step, steps - 1))(action)
            return carry

        lax.fori_loop(0, steps, run, 0)

    def span(step, size):
        return pl.ds(pl.multiple_of(step * size * rows, size * rows), size * rows)

    def whole(source):
        return vec[source].reshape(width, width)

    def rows_of(source):
        if shared:
            return vec[source, blk].reshape(rows, width)
        return vec[source, 0, 0, 0, pl.ds(row0, rows), :]

    own_copy.wait()
    open_line()
    for copy in small_copies:
        copy.wait()
    row_ids = lax.broadcasted_iota(jnp.int32, (rows, width), 0) + row0
    col_ids = lax.broadcasted_iota(jnp.int32, (rows, width), 1)
    vcol = jnp.sum(jnp.where(row_ids == col_ids, vir_ref[...], 0.0), axis=1, keepdims=True)
    base[...] = vcol + vir_ref[...]
    fock_copy.wait()
    left[pl.ds(0, rows), :] = fock[pl.ds(row0, rows), :]

    quad, octo, many = min(4, capacity), min(8, capacity), min(16, capacity)

    def own_left(step):
        for k in range(quad):
            amp_copy(step * quad + k).wait()
        for k in range(quad):
            s = step * quad + k
            both = jnp.dot(left[pl.ds(0, 2 * rows), :], amp[s], preferred_element_type=F32)
            here = pl.ds(pl.multiple_of(s * rows, rows), rows)
            acc[here, :] = both[:rows]
            y_buf[0, here, :] = both[rows:].astype(BF16)
            occ = occ_ref[orbs_ref[0, s]] + occ_ref[orbs_ref[1, s]]
            live = jnp.full((rows, width), s, jnp.int32) < live_ref[0]
            inv[here, :] = jnp.where(live, 1.0 / (base[...] - occ), 0.0)

    def own_right(step):
        here = span(step, quad)
        mine = amp[pl.ds(step * quad, quad), pl.ds(row0, rows), :].reshape(quad * rows, width)
        more = lax.dot_general(mine, fock[...], NT, preferred_element_type=F32)
        more += lax.dot_general(y_buf[0, here, :], whole(blk), NT, preferred_element_type=F32)
        acc[here, :] += more

    left[pl.ds(rows, rows), :] = rows_of(blk)
    phase(capacity // quad, own_left, [(3, functools.partial(until, line_step, 1, 0))])
    phase(capacity // quad, own_right, [
        (k, functools.partial(until, line_step, *which)) for k, which in ((0, (2, 0)), (2, (3, 0)), (3, (1, parts)))])

    for d in range(1, blocks):
        until(line_step, d)
        until(core_step, d)
        left[pl.ds(0, rows), :] = rows_of(vector[d])

        def lefts(step, d=d):
            for k in range(octo):
                s = step * octo + k
                y = jnp.dot(left[pl.ds(0, rows), :], amp[s], preferred_element_type=F32)
                y_buf[d - 1, pl.ds(pl.multiple_of(s * rows, rows), rows), :] = y.astype(BF16)

        if d < blocks - 1:
            hooks = [(plane_step, d + 1, 0), (line_step, min(d + 2, blocks - 1), parts)]
        else:
            hooks = [(plane_step, 1, parts), (plane_step, 2, parts)]
        phase(capacity // octo, lefts, [(k, functools.partial(until, *hook)) for k, hook in enumerate(hooks)])

    for d in range(1, blocks):
        last = d == blocks - 1
        until(core_step, d, parts)

        def rights(step, d=d, last=last):
            here = span(step, many)
            more = lax.dot_general(y_buf[d - 1, here, :], whole(vector[d]), NT, preferred_element_type=F32)
            if last:
                value = ((acc[here, :] + more) * inv[here, :]).astype(BF16)
                out_ref[pl.ds(step * many, many)] = value.reshape(many, rows, width)
            else:
                acc[here, :] += more

        phase(capacity // many, rights)
        until(plane_step, d + 2, parts)

    for d in range(1, blocks):
        for i in range(parts):
            for e in [0] + far(d):
                line_copy(d, i, e).wait_send()
            for e in near(d):
                plane_copy(d, i, e, chip).wait_send()
            if shared:
                core_copy(d, i, core).wait_send()


def solution(mesh):
    owners = mesh.shape["pairs"]
    blocks = mesh.shape["blk"]

    def body(amplitudes, chol_vectors, fock_vv, occ_energy, vir_energy, pair_orbs, live_count):
        capacity, width, _ = amplitudes.shape
        rows = width // blocks
        shared = rows % (16 * owners) == 0
        view = (blocks, owners // 2, 2, rows // owners, width) if shared else (1, 1, 1, width, width)
        parts = view[0].bit_length()
        dma = pltpu.SemaphoreType.DMA
        hbm = pl.BlockSpec(memory_space=pltpu.HBM)
        vmem = pl.BlockSpec(memory_space=pltpu.VMEM)
        n_sends = max(1, view[1] - 1)
        return pl.pallas_call(
            functools.partial(kernel, owners, blocks, shared),
            out_shape=pltpu.VMEM((capacity, rows, width), BF16),
            in_specs=[hbm] * 7,
            out_specs=vmem,
            scratch_shapes=[
                pltpu.SMEM(occ_energy.shape, F32),
                pltpu.VMEM((1, width), F32),
                pltpu.SMEM((2, capacity), jnp.int32),
                pltpu.SMEM(live_count.shape, jnp.int32),
                pltpu.VMEM((capacity, width, width), BF16),
                pltpu.VMEM((blocks,) + view, BF16),
                pltpu.VMEM((width, width), BF16),
                pltpu.VMEM((2 * rows, width), BF16),
                pltpu.VMEM((blocks - 1, capacity * rows, width), BF16),
                pltpu.VMEM((capacity * rows, width), F32),
                pltpu.VMEM((capacity * rows, width), F32),
                pltpu.VMEM((rows, width), F32),
                dma((capacity,)), dma((6,)),
                dma((blocks - 1, parts, n_sends + 1)), dma((blocks - 1, parts, n_sends + 1)),
                dma((blocks - 1, parts, n_sends)), dma((blocks - 1, parts, n_sends)),
                dma((blocks - 1, parts)), dma((blocks - 1, parts)),
            ],
            compiler_params=pltpu.CompilerParams(
                collective_id=0, has_side_effects=True, vmem_limit_bytes=60000 * 1024),
        )(amplitudes, chol_vectors.reshape((1,) + view), fock_vv, occ_energy,
          vir_energy.reshape(1, width), pair_orbs.T, live_count)

    return jax.shard_map(
        body,
        mesh=mesh,
        in_specs=(
            P("pairs", None, None),
            P("blk", None, None),
            P(),
            P(),
            P(),
            P("pairs", None),
            P("pairs"),
        ),
        out_specs=P("pairs", "blk", None),
        check_vma=False,
    )
```

```python
import functools

import jax
import jax.numpy as jnp
from jax import lax
from jax.experimental import pallas as pl
from jax.experimental.pallas import tpu as pltpu
from jax.sharding import PartitionSpec as P

NT = (((1,), (1,)), ((), ()))
LINE_FAR = ((1, 0), (1, 1), (1, 2), (3, 2))
BF16, F32 = jnp.bfloat16, jnp.float32
MESH = pl.DeviceIdType.MESH

def flip(index, mask):
    out = index
    bit = 1
    while bit <= mask:
        if mask & bit:
            out = out + bit - 2 * bit * ((index // bit) % 2)
        bit *= 2
    return out


def kernel(
    owners, blocks, shared,
    amp_hbm, chol_hbm, fock_hbm, occ_hbm, vir_hbm, orbs_hbm, live_hbm,
    out_ref,
    occ_ref, vir_ref, orbs_ref, live_ref,
    amp, vec, fock, left, y_buf, acc, inv, base,
    t_sem, in_sem, zs_sem, zr_sem, ps_sem, pr_sem, cs_sem, cr_sem,
):
    capacity, width, _ = amp_hbm.shape
    rows = width // blocks
    _, inner, chips, _, _, _ = vec.shape
    parts = inner.bit_length()
    own = lax.axis_index("pairs")
    blk = lax.axis_index("blk")
    chip, core = (own // 2, own % 2) if shared else (0, 0)
    row0 = pl.multiple_of(blk * rows, rows)
    def at(pairs, block):
        return {"pairs": pairs, "blk": block}

    barrier = pltpu.get_barrier_semaphore()
    peers = [at(own, flip(blk, d)) for d in range(1, blocks)]
    peers += [at(flip(own, 2 * e), blk) for e in range(1, chips)]
    peers += [at(flip(own, 1), blk)] * int(shared)
    for peer in peers:
        pl.semaphore_signal(barrier, inc=1, device_id=peer, device_id_type=MESH)

    own_copy = pltpu.make_async_copy(chol_hbm.at[0], vec.at[blk], in_sem.at[0])
    fock_copy = pltpu.make_async_copy(fock_hbm, fock, in_sem.at[1])
    small_copies = [
        pltpu.make_async_copy(source, target, in_sem.at[2 + i])
        for i, (source, target) in enumerate(
            [(occ_hbm, occ_ref), (vir_hbm, vir_ref), (orbs_hbm, orbs_ref), (live_hbm, live_ref)])
    ]

    def amp_copy(s):
        return pltpu.make_async_copy(amp_hbm.at[s], amp.at[s], t_sem.at[s])

    own_copy.start()
    fock_copy.start()
    for copy in small_copies:
        copy.start()
    for s in range(capacity):
        amp_copy(s).start()

    vector = [flip(blk, d) for d in range(blocks)]

    extents = [2 ** max(0, i - 1) for i in range(parts)]
    starts = [
        [flip(receiver // extent, min(1, i)) * extent if inner > 1 else 0 for i, extent in enumerate(extents)]
        for receiver in vector]
    chip_peers = [flip(chip, e) for e in range(chips)]
    own_peers = [flip(own, 2 * e) for e in range(chips)]
    twin, other = flip(own, 1), 1 - core

    def part(d, i):
        return pl.ds(starts[d][i], extents[i])

    def far(d, i):
        return [e for e in range(1, chips) if e & (e - 1)] if (d, i) in LINE_FAR else []

    def near(d, i):
        return [e for e in range(chips - 1, 0, -1) if e not in far(d, i)]

    def line_copy(d, i, e=0):
        piece = vec.at[blk, part(d, i), chip_peers[e], core]
        return pltpu.make_async_remote_copy(
            src_ref=piece, dst_ref=piece, send_sem=zs_sem.at[d - 1, i, e], recv_sem=zr_sem.at[d - 1, i, e],
            device_id=at(own, vector[d]), device_id_type=MESH)

    def line_arrival(d, i, e=0):
        piece = vec.at[vector[d], part(0, i), chip_peers[e], core]
        return pltpu.make_async_remote_copy(
            src_ref=piece, dst_ref=piece, send_sem=zs_sem.at[d - 1, i, e], recv_sem=zr_sem.at[d - 1, i, e],
            device_id=at(own, vector[d]), device_id_type=MESH)

    def plane_copy(d, i, e, source):
        piece = vec.at[vector[d], part(0, i), source, core]
        return pltpu.make_async_remote_copy(
            src_ref=piece, dst_ref=piece, send_sem=ps_sem.at[d - 1, i, e - 1], recv_sem=pr_sem.at[d - 1, i, e - 1],
            device_id=at(own_peers[e], blk), device_id_type=MESH)

    def core_copy(d, i, side):
        piece = vec.at[vector[d], part(0, i), :, side]
        return pltpu.make_async_remote_copy(
            src_ref=piece, dst_ref=piece, send_sem=cs_sem.at[d - 1, i], recv_sem=cr_sem.at[d - 1, i],
            device_id=at(twin, blk), device_id_type=MESH)

    def open_line():
        pl.semaphore_wait(barrier, len(peers))
        for d in range(1, blocks):
            for e in [0] + far(d, 0):
                line_copy(d, 0, e).start()
        for d in range(1, blocks):
            for i in range(1, parts):
                for e in [0] + far(d, i):
                    line_copy(d, i, e).start()

    def line_step(d, i):
        line_arrival(d, i).wait_recv()
        for e in near(d, i):
            plane_copy(d, i, e, chip).start()

    def plane_step(d, i):
        for e in far(d, i):
            line_arrival(d, i, e).wait_recv()
        for e in near(d, i):
            plane_copy(d, i, e, chip_peers[e]).wait_recv()
        core_copy(d, i, core).start()

    def core_step(d, i):
        core_copy(d, i, other).wait_recv()

    def rest(kind, d):
        return [(kind, d, i) for i in range(1, parts)]

    steps_left = [(line_step, d, 0) for d in range(1, blocks)] + rest(line_step, 1)
    for d in range(1, blocks):
        steps_left += [(plane_step, d, 0)] * int(shared) + rest(line_step, d + 1) * int(d + 1 < blocks)
        steps_left += [(core_step, d, 0)] * int(shared)
    for d in range(1, blocks):
        steps_left += rest(plane_step, d) + rest(core_step, d)

    def until(kind, d, i=0):
        i = min(i, parts - 1)
        if (kind, d, i) in steps_left:
            taken = steps_left.index((kind, d, i)) + 1
            for step, e, k in steps_left[:taken]:
                step(e, k)
            del steps_left[:taken]

    def phase(steps, body, hooks=()):
        def run(step, carry):
            body(step)
            for at_step, action in hooks:
                pl.when(step == min(at_step, steps - 1))(action)
            return carry

        lax.fori_loop(0, steps, run, 0)

    def span(step, size):
        return pl.ds(pl.multiple_of(step * size * rows, size * rows), size * rows)

    def whole(source):
        return vec[source].reshape(width, width)

    def rows_of(source):
        if shared:
            return vec[source, blk].reshape(rows, width)
        return vec[source, 0, 0, 0, pl.ds(row0, rows), :]

    for copy in small_copies:
        copy.wait()
    row_ids = lax.broadcasted_iota(jnp.int32, (rows, width), 0) + row0
    col_ids = lax.broadcasted_iota(jnp.int32, (rows, width), 1)
    vcol = jnp.sum(jnp.where(row_ids == col_ids, vir_ref[...], 0.0), axis=1, keepdims=True)
    base[...] = vcol + vir_ref[...]
    fock_copy.wait()
    left[pl.ds(0, rows), :] = fock[pl.ds(row0, rows), :]

    quad, octo, many = min(4, capacity), min(8, capacity), min(16, capacity)

    def own_left(step):
        for k in range(quad):
            amp_copy(step * quad + k).wait()
        for k in range(quad):
            s = step * quad + k
            both = jnp.dot(left[pl.ds(0, 2 * rows), :], amp[s], preferred_element_type=F32)
            here = pl.ds(pl.multiple_of(s * rows, rows), rows)
            acc[here, :] = both[:rows]
            y_buf[0, here, :] = both[rows:].astype(BF16)
            occ = occ_ref[orbs_ref[0, s]] + occ_ref[orbs_ref[1, s]]
            live = jnp.full((rows, width), s, jnp.int32) < live_ref[0]
            inv[here, :] = jnp.where(live, 1.0 / (base[...] - occ), 0.0)

    def own_right(step):
        here = span(step, octo)
        mine = amp[pl.ds(step * octo, octo), pl.ds(row0, rows), :].reshape(octo * rows, width)
        more = lax.dot_general(mine, fock[...], NT, preferred_element_type=F32)
        more += lax.dot_general(y_buf[0, here, :], whole(blk), NT, preferred_element_type=F32)
        acc[here, :] += more

    own_copy.wait()
    left[pl.ds(rows, rows), :] = rows_of(blk)
    open_line()
    phase(capacity // quad, own_left, [(3, functools.partial(until, line_step, 1, 0))])
    phase(capacity // octo, own_right, [(0, functools.partial(until, line_step, 2, 0)), (1, functools.partial(until, line_step, 3, 0))])

    for d in range(1, blocks):
        until(line_step, d)
        until(core_step, d)
        left[pl.ds(0, rows), :] = rows_of(vector[d])

        def lefts(step, d=d):
            for k in range(octo):
                s = step * octo + k
                y = jnp.dot(left[pl.ds(0, rows), :], amp[s], preferred_element_type=F32)
                y_buf[d - 1, pl.ds(pl.multiple_of(s * rows, rows), rows), :] = y.astype(BF16)

        if d < blocks - 1:
            hooks = [(plane_step, d + 1, 0), (core_step, d + 1, 0)]
        else:
            hooks = [(plane_step, 1, parts), (plane_step, 2, parts)]
        phase(capacity // octo, lefts, [(k, functools.partial(until, *hook)) for k, hook in enumerate(hooks)])

    for d in range(1, blocks):
        last = d == blocks - 1
        until(core_step, d, parts)

        def rights(step, d=d, last=last):
            here = span(step, many)
            more = lax.dot_general(y_buf[d - 1, here, :], whole(vector[d]), NT, preferred_element_type=F32)
            if last:
                value = ((acc[here, :] + more) * inv[here, :]).astype(BF16)
                out_ref[pl.ds(step * many, many)] = value.reshape(many, rows, width)
            else:
                acc[here, :] += more

        phase(capacity // many, rights)
        until(plane_step, d + 2, parts)

    for d in range(1, blocks):
        for i in range(parts):
            for e in [0] + far(d, i):
                line_copy(d, i, e).wait_send()
            for e in near(d, i):
                plane_copy(d, i, e, chip).wait_send()
            if shared:
                core_copy(d, i, core).wait_send()


def solution(mesh):
    owners = mesh.shape["pairs"]
    blocks = mesh.shape["blk"]

    def body(amplitudes, chol_vectors, fock_vv, occ_energy, vir_energy, pair_orbs, live_count):
        capacity, width, _ = amplitudes.shape
        rows = width // blocks
        shared = rows % (16 * owners) == 0
        view = (blocks, owners // 2, 2, rows // owners, width) if shared else (1, 1, 1, width, width)
        parts = view[0].bit_length()
        dma = pltpu.SemaphoreType.DMA
        hbm = pl.BlockSpec(memory_space=pltpu.HBM)
        vmem = pl.BlockSpec(memory_space=pltpu.VMEM)
        n_sends = max(1, view[1] - 1)
        return pl.pallas_call(
            functools.partial(kernel, owners, blocks, shared),
            out_shape=pltpu.VMEM((capacity, rows, width), BF16),
            in_specs=[hbm] * 7,
            out_specs=vmem,
            scratch_shapes=[
                pltpu.SMEM(occ_energy.shape, F32),
                pltpu.VMEM((1, width), F32),
                pltpu.SMEM((2, capacity), jnp.int32),
                pltpu.SMEM(live_count.shape, jnp.int32),
                pltpu.VMEM((capacity, width, width), BF16),
                pltpu.VMEM((blocks,) + view, BF16),
                pltpu.VMEM((width, width), BF16),
                pltpu.VMEM((2 * rows, width), BF16),
                pltpu.VMEM((blocks - 1, capacity * rows, width), BF16),
                pltpu.VMEM((capacity * rows, width), F32),
                pltpu.VMEM((capacity * rows, width), F32),
                pltpu.VMEM((rows, width), F32),
                dma((capacity,)), dma((6,)),
                dma((blocks - 1, parts, n_sends + 1)), dma((blocks - 1, parts, n_sends + 1)),
                dma((blocks - 1, parts, n_sends)), dma((blocks - 1, parts, n_sends)),
                dma((blocks - 1, parts)), dma((blocks - 1, parts)),
            ],
            compiler_params=pltpu.CompilerParams(
                collective_id=0, has_side_effects=True, vmem_limit_bytes=60000 * 1024),
        )(amplitudes, chol_vectors.reshape((1,) + view), fock_vv, occ_energy,
          vir_energy.reshape(1, width), pair_orbs.T, live_count)

    return jax.shard_map(
        body,
        mesh=mesh,
        in_specs=(
            P("pairs", None, None),
            P("blk", None, None),
            P(),
            P(),
            P(),
            P("pairs", None),
            P("pairs"),
        ),
        out_specs=P("pairs", "blk", None),
        check_vma=False,
    )
```
